32 devices in a mesh: seq: 8 (over y, x, core), head: 4 (over z).
Axes of the slice: x: 2, y: 2, z: 4, core: 2. Of those that a mesh axis runs over, the one named last changes fastest.
Arguments:
- teacher_query: bfloat16 [7168, 1024], P(('seq', 'head')), may hold values from -96 to 96
- teacher_key: bfloat16 [7168, 1024], P(('seq', 'head')), may hold values from -96 to 96
- teacher_value: bfloat16 [7168, 1024], P(('seq', 'head')), may hold values from -96 to 96
- student_query: bfloat16 [7168, 768], P(('seq', 'head')), may hold values from -96 to 96
- student_key: bfloat16 [7168, 768], P(('seq', 'head')), may hold values from -96 to 96
- student_value: bfloat16 [7168, 768], P(('seq', 'head')), may hold values from -96 to 96
Outputs:
- grad_query: bfloat16 [7168, 768], P(('seq', 'head'))
- grad_key: bfloat16 [7168, 768], P(('seq', 'head'))
- grad_value: bfloat16 [7168, 768], P(('seq', 'head'))
- loss: float32 [], replicated
The draws below stay inside these ranges and needn't reach their ends.
All inputs are finite; a program needn't handle non-finite values.
Results may differ from the reference program's by a relative error of at most 0.0051.
Values may be sent and summed in bfloat16 or wider, within the bound.
A program may use at most 128 MiB of HBM per device.

```python
import jax
import jax.numpy as jnp
from jax import lax

HEADS = 16
TD = 64
SD = 48
L = 7168


def shared_draw(key, width, salt):
    base = jax.random.fold_in(key, salt)
    query = jnp.clip(jax.random.normal(jax.random.fold_in(base, 1), (L, width), jnp.float32), -5.0, 5.0)
    keys = jnp.clip(jax.random.normal(jax.random.fold_in(base, 2), (L, width), jnp.float32), -5.0, 5.0)
    values = jnp.clip(jax.random.normal(jax.random.fold_in(base, 3), (L, width), jnp.float32), -5.0, 5.0)
    return (query, keys, values)


def draw_teacher_query(key, part):
    return shared_draw(key, HEADS * TD, 11)[0].astype(jnp.bfloat16)


def draw_teacher_key(key, part):
    return shared_draw(key, HEADS * TD, 11)[1].astype(jnp.bfloat16)


def draw_teacher_value(key, part):
    return shared_draw(key, HEADS * TD, 11)[2].astype(jnp.bfloat16)


def draw_student_query(key, part):
    return shared_draw(key, HEADS * SD, 23)[0].astype(jnp.bfloat16)


def draw_student_key(key, part):
    return shared_draw(key, HEADS * SD, 23)[1].astype(jnp.bfloat16)


def draw_student_value(key, part):
    return shared_draw(key, HEADS * SD, 23)[2].astype(jnp.bfloat16)


def setup_inputs(seed: int = 0) -> dict:
    streams_of = jax.random.split(jax.random.key(seed), 7)
    return {
        "teacher_query": draw_teacher_query(jax.random.fold_in(streams_of[6], 71), 0),
        "teacher_key": draw_teacher_key(jax.random.fold_in(streams_of[6], 71), 0),
        "teacher_value": draw_teacher_value(jax.random.fold_in(streams_of[6], 71), 0),
        "student_query": draw_student_query(jax.random.fold_in(streams_of[6], 71), 0),
        "student_key": draw_student_key(jax.random.fold_in(streams_of[6], 71), 0),
        "student_value": draw_student_value(jax.random.fold_in(streams_of[6], 71), 0),
    }


def per_head(arrays):
    teach_q, teach_k, teach_v, stud_q, stud_k, stud_v = arrays
    tscale = TD ** -0.5
    sscale = SD ** -0.5
    block = min(512, L)
    turns = L // block

    def one_block(carry, index):
        key_acc, value_acc, total = carry
        begin = (index * block).astype(jnp.int32)
        row_tq = lax.dynamic_slice_in_dim(teach_q, begin, block, 0)
        row_tv = lax.dynamic_slice_in_dim(teach_v, begin, block, 0)
        row_sq = lax.dynamic_slice_in_dim(stud_q, begin, block, 0)
        row_sv = lax.dynamic_slice_in_dim(stud_v, begin, block, 0)
        logit_a = jnp.dot(row_tq, teach_k.T, preferred_element_type=jnp.float32) * tscale
        logit_b = jnp.dot(row_tv, teach_v.T, preferred_element_type=jnp.float32) * tscale
        logit_c = jnp.dot(row_sq, stud_k.T, preferred_element_type=jnp.float32) * sscale
        logit_e = jnp.dot(row_sv, stud_v.T, preferred_element_type=jnp.float32) * sscale
        log_a = logit_a - jax.nn.logsumexp(logit_a, axis=1, keepdims=True)
        log_b = logit_b - jax.nn.logsumexp(logit_b, axis=1, keepdims=True)
        log_c = logit_c - jax.nn.logsumexp(logit_c, axis=1, keepdims=True)
        log_e = logit_e - jax.nn.logsumexp(logit_e, axis=1, keepdims=True)
        prob_a = jnp.exp(log_a)
        prob_b = jnp.exp(log_b)
        total = total + jnp.sum(prob_a * (log_a - log_c)) + jnp.sum(prob_b * (log_b - log_e))
        grad_qk = (jnp.exp(log_c) - prob_a).astype(jnp.bfloat16)
        grad_vv = (jnp.exp(log_e) - prob_b).astype(jnp.bfloat16)
        row_dq = jnp.dot(grad_qk, stud_k, preferred_element_type=jnp.float32) * sscale
        row_dv = jnp.dot(grad_vv, stud_v, preferred_element_type=jnp.float32) * sscale
        key_acc = key_acc + jnp.dot(grad_qk.T, row_sq, preferred_element_type=jnp.float32) * sscale
        value_acc = value_acc + jnp.dot(grad_vv.T, row_sv, preferred_element_type=jnp.float32) * sscale
        return (key_acc, value_acc, total), (row_dq, row_dv)

    start = (jnp.zeros((L, SD), jnp.float32), jnp.zeros((L, SD), jnp.float32), jnp.zeros((), jnp.float32))
    (key_acc, value_acc, total), (rows_dq, rows_dv) = lax.scan(one_block, start, jnp.arange(turns, dtype=jnp.int32))
    grad_q = rows_dq.reshape(L, SD)
    grad_v = rows_dv.reshape(L, SD) + value_acc
    return grad_q, key_acc, grad_v, total


def split_heads(array, width):
    return array.reshape(L, HEADS, width).transpose(1, 0, 2)


def join_heads(array):
    return array.transpose(1, 0, 2).reshape(L, HEADS * SD).astype(jnp.bfloat16)


def reference(teacher_query, teacher_key, teacher_value, student_query, student_key, student_value):
    arrays = (split_heads(teacher_query, TD), split_heads(teacher_key, TD), split_heads(teacher_value, TD),
              split_heads(student_query, SD), split_heads(student_key, SD), split_heads(student_value, SD))
    grad_q, grad_k, grad_v, totals = lax.map(per_head, arrays)
    loss = jnp.sum(totals) / (HEADS * L)
    return join_heads(grad_q), join_heads(grad_k), join_heads(grad_v), loss
```

```python
import functools
import math

import jax
import jax.numpy as jnp
from jax import lax
from jax.experimental import pallas as pl
from jax.experimental.pallas import tpu as pltpu
from jax.sharding import PartitionSpec as P

HEADS = 16
TD = 64
SD = 48
RB = 128
LIMIT = 100.0
LOG2E = math.log2(math.e)
LN2 = math.log(2.0)
F32 = jnp.float32
BF16 = jnp.bfloat16


def pick(count, options):
    for size in options:
        if count % size == 0:
            return size
    return count


def fold(x):
    return jnp.sum(x.reshape(x.shape[0] // 8, 8, x.shape[1]), axis=0)


def fold_max(x):
    return jnp.max(x.reshape(x.shape[0] // 8, 8, x.shape[1]), axis=0)


def kernel(q_ref, k_ref, dq_ref, dk_ref, kl_ref, kt_ref, cm_ref, e_ref, st_ref):
    count = k_ref.shape[0]
    first = pick(count, (512, 256, 128, 64, 32, 16, 8))
    second = pick(count, (1024, 512, 256, 128))
    tfac = TD ** (-0.5) * LOG2E
    sfac = SD ** (-0.5) * LOG2E
    sscale = SD ** (-0.5)

    @pl.when(pl.program_id(1) == 0)
    def _():
        dk_ref[...] = jnp.zeros_like(dk_ref)
        part = pick(count, (1024, 512, 256, 128))

        def prepare(i, tops):
            here = pl.ds(pl.multiple_of(i * part, part), part)
            x = k_ref[here, :].astype(F32)
            kt_ref[64:128, here] = x[:, :128].T[64:, :].astype(BF16)
            kt_ref[0:64, here] = x[:, 128:].T[64:, :].astype(BF16)
            return jnp.maximum(tops, fold_max(jnp.abs(x)))

        tops = lax.fori_loop(0, count // part, prepare, jnp.zeros((8, 256), F32))
        tops = jnp.max(tops, axis=0, keepdims=True)
        cm_ref[...] = jnp.broadcast_to(tops, cm_ref.shape)

    q = q_ref[...].astype(F32)
    lane = lax.broadcasted_iota(jnp.int32, (RB, 128), 1)
    row = lax.broadcasted_iota(jnp.int32, (128, RB), 0)

    def weights(block):
        t = block.T
        t = jnp.concatenate(
            [jnp.where(row < TD, t, 0.0), jnp.where(row < TD, 0.0, t)], axis=1
        )
        return t

    raw_k, raw_v = weights(q[:, :128]), weights(q[:, 128:])
    col = lax.broadcasted_iota(jnp.int32, (1, 256), 1)
    factor = jnp.where(col < RB, tfac, sfac)
    full_k, full_v = raw_k * factor, raw_v * factor
    bound_k = jnp.dot(
        cm_ref[:, :128].astype(BF16), jnp.abs(raw_k).astype(BF16), preferred_element_type=F32
    )
    bound_v = jnp.dot(
        cm_ref[:, 128:].astype(BF16), jnp.abs(raw_v).astype(BF16), preferred_element_type=F32
    )
    bound = jnp.max(jnp.maximum(bound_k * factor, bound_v * factor))

    zero = jnp.zeros((8, RB), F32)

    def total(x):
        return jnp.broadcast_to(jnp.sum(x, axis=0, keepdims=True), x.shape)

    @pl.when(bound <= LIMIT)
    def _():
        def split(w):
            high = w.astype(BF16)
            low = (w - high.astype(F32)).astype(BF16)
            return jnp.concatenate([high, low], axis=0)

        wk, wv = split(full_k), split(full_v)

        def step(i, carry):
            za, zc, s, zb, ze, u = carry
            here = pl.ds(pl.multiple_of(i * first, first), first)
            xk = k_ref[here, :128]
            xv = k_ref[here, 128:]
            lk = jnp.dot(jnp.concatenate([xk, xk], axis=1), wk, preferred_element_type=F32)
            lv = jnp.dot(jnp.concatenate([xv, xv], axis=1), wv, preferred_element_type=F32)
            a, c, b, e = lk[:, :RB], lk[:, RB:], lv[:, :RB], lv[:, RB:]
            pa, pc, pb, pe = jnp.exp2(a), jnp.exp2(c), jnp.exp2(b), jnp.exp2(e)
            e_ref[here, 0:128] = pa.astype(e_ref.dtype)
            e_ref[here, 128:256] = pc.astype(e_ref.dtype)
            e_ref[here, 256:384] = pb.astype(e_ref.dtype)
            e_ref[here, 384:512] = pe.astype(e_ref.dtype)
            return (
                za + fold(pa), zc + fold(pc), s + fold(pa * (a - c)),
                zb + fold(pb), ze + fold(pe), u + fold(pb * (b - e)),
            )

        out = lax.fori_loop(0, count // first, step, (zero,) * 6)
        for n, value in enumerate(out):
            st_ref[n] = total(value)

    @pl.when(jnp.logical_not(bound <= LIMIT))
    def _():
        wk, wv = raw_k.astype(BF16), raw_v.astype(BF16)

        def blocks(i):
            here = pl.ds(pl.multiple_of(i * first, first), first)
            lk = jnp.dot(k_ref[here, :128], wk, preferred_element_type=F32)
            lv = jnp.dot(k_ref[here, 128:], wv, preferred_element_type=F32)
            return here, (
                lk[:, :RB] * tfac, lk[:, RB:] * sfac, lv[:, :RB] * tfac, lv[:, RB:] * sfac
            )

        def peak(i, tops):
            _, parts = blocks(i)
            return tuple(jnp.maximum(t, fold_max(p)) for t, p in zip(tops, parts))

        tops = lax.fori_loop(
            0, count // first, peak, (jnp.full((8, RB), -3e38, F32),) * 4
        )
        tops = tuple(jnp.max(t, axis=0, keepdims=True) for t in tops)

        def step(i, carry):
            za, zc, s, zb, ze, u = carry
            here, parts = blocks(i)
            a, c, b, e = (p - t for p, t in zip(parts, tops))
            pa, pc, pb, pe = jnp.exp2(a), jnp.exp2(c), jnp.exp2(b), jnp.exp2(e)
            e_ref[here, 0:128] = pa.astype(e_ref.dtype)
            e_ref[here, 128:256] = pc.astype(e_ref.dtype)
            e_ref[here, 256:384] = pb.astype(e_ref.dtype)
            e_ref[here, 384:512] = pe.astype(e_ref.dtype)
            return (
                za + fold(pa), zc + fold(pc), s + fold(pa * (a - c)),
                zb + fold(pb), ze + fold(pe), u + fold(pb * (b - e)),
            )

        out = lax.fori_loop(0, count // first, step, (zero,) * 6)
        for n, value in enumerate(out):
            st_ref[n] = total(value)

    za, zc, s, zb, ze, u = (st_ref[n] for n in range(6))
    kl_ref[...] = (
        s / za - jnp.log2(za) + jnp.log2(zc) + u / zb - jnp.log2(zb) + jnp.log2(ze)
    ) * LN2
    ia, ic, ib, ie = (1.0 / z[0:1, :] for z in (za, zc, zb, ze))

    only_k = jnp.where(lane < TD, 0.0, q[:, :128])
    only_v = pltpu.roll(jnp.where(lane < TD, 0.0, q[:, 128:]), 64, 1)
    wd = jnp.concatenate([only_k, only_v], axis=0).astype(BF16)

    def grads(i, acc):
        here = pl.ds(pl.multiple_of(i * second, second), second)
        gk = (e_ref[here, 128:256] * ic - e_ref[here, 0:128] * ia).astype(BF16)
        gv = (e_ref[here, 384:512] * ie - e_ref[here, 256:384] * ib).astype(BF16)
        g = jnp.concatenate([gk, gv], axis=1)
        dk_ref[here, :] += jnp.dot(g, wd, preferred_element_type=F32)
        return acc + jnp.dot(kt_ref[:, here], g, preferred_element_type=F32)

    acc = lax.fori_loop(0, count // second, grads, jnp.zeros((128, 256), F32))
    d = jnp.where(row < TD, acc[:, RB:], acc[:, :RB])
    dq_ref[...] = d.T * sscale

    @pl.when(pl.program_id(1) == pl.num_programs(1) - 1)
    def _():
        dk_ref[...] = dk_ref[...] * sscale


def relation(q, k, local_heads):
    rows, count = q.shape[0], k.shape[0]
    turns = rows // RB
    return pl.pallas_call(
        kernel,
        out_shape=(
            jax.ShapeDtypeStruct((rows, local_heads * 128), F32),
            jax.ShapeDtypeStruct((count, local_heads * 128), F32),
            jax.ShapeDtypeStruct((8, local_heads * rows), F32),
        ),
        grid_spec=pltpu.PrefetchScalarGridSpec(
            num_scalar_prefetch=0,
            grid=(local_heads, turns),
            in_specs=[
                pl.BlockSpec((RB, 256), lambda h, r: (r, h)),
                pl.BlockSpec((count, 256), lambda h, r: (0, h)),
            ],
            out_specs=[
                pl.BlockSpec((RB, 128), lambda h, r: (r, h)),
                pl.BlockSpec((count, 128), lambda h, r: (0, h)),
                pl.BlockSpec((8, RB), lambda h, r: (0, h * turns + r)),
            ],
            scratch_shapes=[
                pltpu.VMEM((128, count), BF16),
                pltpu.VMEM((8, 256), F32),
                pltpu.VMEM((count, 512), F32),
                pltpu.VMEM((6, 8, RB), F32),
            ],
        ),
        compiler_params=pltpu.CompilerParams(
            dimension_semantics=("arbitrary", "arbitrary"), vmem_limit_bytes=58 << 20
        ),
        cost_estimate=pl.CostEstimate(
            flops=int(local_heads * rows * count * 2 * 1024),
            bytes_accessed=int(local_heads * count * 1024),
            transcendentals=int(local_heads * rows * count * 4),
        ),
    )(q, k)


def on_device(teacher_query, teacher_key, teacher_value, student_query, student_key, student_value):
    tokens = teacher_query.shape[0]

    def pack(teacher, student):
        return jnp.concatenate(
            [
                teacher.reshape(tokens, HEADS, TD),
                student.reshape(tokens, HEADS, SD),
                jnp.zeros((tokens, HEADS, 128 - TD - SD), BF16),
            ],
            axis=2,
        )

    packed = jnp.concatenate(
        [
            pack(teacher_query, student_query),
            pack(teacher_key, student_key),
            pack(teacher_value, student_value),
        ],
        axis=2,
    ).reshape(tokens, HEADS * 384)
    mine = lax.all_to_all(packed, "head", split_axis=1, concat_axis=0, tiled=True)
    rows = mine.shape[0]
    local_heads = mine.shape[1] // 384
    total_rows = rows * lax.axis_size("seq")
    mine = mine.reshape(rows, local_heads, 384)
    keys = mine[:, :, 128:].reshape(rows, local_heads * 256)
    queries = jnp.concatenate([mine[:, :, :128], mine[:, :, 256:]], axis=2)
    queries = queries.reshape(rows, local_heads * 256)
    padded = -(-rows // RB) * RB
    queries = jnp.pad(queries, ((0, padded - rows), (0, 0)))
    keys = lax.all_gather(keys, "seq", axis=0, tiled=True)
    dq, dk, kl = relation(queries, keys, local_heads)
    kl = jnp.sum(kl[0].reshape(local_heads, padded)[:, :rows])
    loss = lax.psum(kl, ("seq", "head")) / (HEADS * total_rows)

    dk = dk.reshape(total_rows, local_heads, 128)
    dk = jnp.concatenate([dk[:, :, TD : TD + SD], dk[:, :, :SD]], axis=2)
    dk = dk.reshape(total_rows, local_heads * 2 * SD)
    owned = lax.psum_scatter(dk, "seq", scatter_dimension=0, tiled=True)
    owned = owned.reshape(rows, local_heads, 2 * SD)
    dq = dq[:rows].reshape(rows, local_heads, 128)
    out = jnp.concatenate(
        [dq[:, :, TD : TD + SD], owned[:, :, :SD], owned[:, :, SD:] + dq[:, :, :SD]], axis=2
    ).astype(BF16)
    out = out.reshape(rows, local_heads * 3 * SD)
    out = lax.all_to_all(out, "head", split_axis=0, concat_axis=1, tiled=True)
    out = out.reshape(tokens, HEADS, 3, SD)
    return tuple(out[:, :, n].reshape(tokens, HEADS * SD) for n in range(3)) + (loss,)


def solution(mesh):
    spec = P(("seq", "head"), None)
    return jax.shard_map(
        on_device, mesh=mesh, in_specs=(spec,) * 6, out_specs=(spec, spec, spec, P()),
        check_vma=False,
    )
```

```python
import functools
import math

import jax
import jax.numpy as jnp
from jax import lax
from jax.experimental import pallas as pl
from jax.experimental.pallas import tpu as pltpu
from jax.sharding import PartitionSpec as P

HEADS = 16
TD = 64
SD = 48
RB = 128
LIMIT = 100.0
LOG2E = math.log2(math.e)
LN2 = math.log(2.0)
F32 = jnp.float32
BF16 = jnp.bfloat16


def pick(count, options):
    for size in options:
        if count % size == 0:
            return size
    return count


def fold(x):
    return jnp.sum(x.reshape(x.shape[0] // 8, 8, x.shape[1]), axis=0)


def fold_max(x):
    return jnp.max(x.reshape(x.shape[0] // 8, 8, x.shape[1]), axis=0)


def kernel(rows, q_ref, k_ref, dq_ref, dk_ref, kt_ref, cm_ref, e_ref, st_ref, kl_ref):
    count = k_ref.shape[0]
    first = pick(count, (1792, 1024, 512, 256, 128))
    second = pick(count, (3584, 1024, 512, 256, 128))
    tfac = TD ** (-0.5) * LOG2E
    sfac = SD ** (-0.5) * LOG2E
    sscale = SD ** (-0.5)

    @pl.when(pl.program_id(1) == 0)
    def _():
        dk_ref[...] = jnp.zeros_like(dk_ref)
        part = pick(count, (1024, 512, 256, 128))

        def prepare(i, tops):
            here = pl.ds(pl.multiple_of(i * part, part), part)
            x = k_ref[here, :].astype(F32)
            kt_ref[64:128, here] = x[:, :128].T[64:, :].astype(BF16)
            kt_ref[0:64, here] = x[:, 128:].T[64:, :].astype(BF16)
            return jnp.maximum(tops, fold_max(jnp.abs(x)))

        tops = lax.fori_loop(0, count // part, prepare, jnp.zeros((8, 256), F32))
        tops = jnp.max(tops, axis=0, keepdims=True)
        cm_ref[...] = jnp.broadcast_to(tops, cm_ref.shape)

    q = q_ref[...].astype(F32)
    lane = lax.broadcasted_iota(jnp.int32, (RB, 128), 1)
    row = lax.broadcasted_iota(jnp.int32, (128, RB), 0)

    def weights(block):
        t = block.T
        t = jnp.concatenate(
            [jnp.where(row < TD, t, 0.0), jnp.where(row < TD, 0.0, t)], axis=1
        )
        return t

    raw_k, raw_v = weights(q[:, :128]), weights(q[:, 128:])
    col = lax.broadcasted_iota(jnp.int32, (1, 256), 1)
    factor = jnp.where(col < RB, tfac, sfac)
    full_k, full_v = raw_k * factor, raw_v * factor
    bound_k = jnp.dot(
        cm_ref[:, :128].astype(BF16), jnp.abs(raw_k).astype(BF16), preferred_element_type=F32
    )
    bound_v = jnp.dot(
        cm_ref[:, 128:].astype(BF16), jnp.abs(raw_v).astype(BF16), preferred_element_type=F32
    )
    bound = jnp.max(jnp.maximum(bound_k * factor, bound_v * factor))

    zero = jnp.zeros((8, RB), F32)

    def total(x):
        return jnp.broadcast_to(jnp.sum(x, axis=0, keepdims=True), x.shape)

    @pl.when(bound <= LIMIT)
    def _():
        def split(w):
            high = w.astype(BF16)
            low = (w - high.astype(F32)).astype(BF16)
            return jnp.concatenate([high, low], axis=0)

        wk, wv = split(full_k), split(full_v)

        def step(i, carry):
            za, zc, s, zb, ze, u = carry
            here = pl.ds(pl.multiple_of(i * first, first), first)
            xk = k_ref[here, :128]
            xv = k_ref[here, 128:]
            lk = jnp.dot(jnp.concatenate([xk, xk], axis=1), wk, preferred_element_type=F32)
            lv = jnp.dot(jnp.concatenate([xv, xv], axis=1), wv, preferred_element_type=F32)
            a, c, b, e = lk[:, :RB], lk[:, RB:], lv[:, :RB], lv[:, RB:]
            pa, pc, pb, pe = jnp.exp2(a), jnp.exp2(c), jnp.exp2(b), jnp.exp2(e)
            e_ref[here, 0:128] = pa.astype(e_ref.dtype)
            e_ref[here, 128:256] = pc.astype(e_ref.dtype)
            e_ref[here, 256:384] = pb.astype(e_ref.dtype)
            e_ref[here, 384:512] = pe.astype(e_ref.dtype)
            return (
                za + fold(pa), zc + fold(pc), s + fold(pa * (a - c)),
                zb + fold(pb), ze + fold(pe), u + fold(pb * (b - e)),
            )

        out = lax.fori_loop(0, count // first, step, (zero,) * 6)
        for n, value in enumerate(out):
            st_ref[n] = total(value)

    @pl.when(jnp.logical_not(bound <= LIMIT))
    def _():
        wk, wv = raw_k.astype(BF16), raw_v.astype(BF16)

        def blocks(i):
            here = pl.ds(pl.multiple_of(i * first, first), first)
            lk = jnp.dot(k_ref[here, :128], wk, preferred_element_type=F32)
            lv = jnp.dot(k_ref[here, 128:], wv, preferred_element_type=F32)
            return here, (
                lk[:, :RB] * tfac, lk[:, RB:] * sfac, lv[:, :RB] * tfac, lv[:, RB:] * sfac
            )

        def peak(i, tops):
            _, parts = blocks(i)
            return tuple(jnp.maximum(t, fold_max(p)) for t, p in zip(tops, parts))

        tops = lax.fori_loop(
            0, count // first, peak, (jnp.full((8, RB), -3e38, F32),) * 4
        )
        tops = tuple(jnp.max(t, axis=0, keepdims=True) for t in tops)

        def step(i, carry):
            za, zc, s, zb, ze, u = carry
            here, parts = blocks(i)
            a, c, b, e = (p - t for p, t in zip(parts, tops))
            pa, pc, pb, pe = jnp.exp2(a), jnp.exp2(c), jnp.exp2(b), jnp.exp2(e)
            e_ref[here, 0:128] = pa.astype(e_ref.dtype)
            e_ref[here, 128:256] = pc.astype(e_ref.dtype)
            e_ref[here, 256:384] = pb.astype(e_ref.dtype)
            e_ref[here, 384:512] = pe.astype(e_ref.dtype)
            return (
                za + fold(pa), zc + fold(pc), s + fold(pa * (a - c)),
                zb + fold(pb), ze + fold(pe), u + fold(pb * (b - e)),
            )

        out = lax.fori_loop(0, count // first, step, (zero,) * 6)
        for n, value in enumerate(out):
            st_ref[n] = total(value)

    za, zc, s, zb, ze, u = (st_ref[n] for n in range(6))
    kl = (s / za - jnp.log2(za) + jnp.log2(zc) + u / zb - jnp.log2(zb) + jnp.log2(ze)) * LN2
    place = pl.program_id(1) * RB + lax.broadcasted_iota(jnp.int32, (8, RB), 1)
    kl = jnp.sum(jnp.where(place < rows, kl, 0.0)) * 0.125
    kl_ref[0, 0] = jnp.where(pl.program_id(1) == 0, 0.0, kl_ref[0, 0]) + kl
    ia, ic, ib, ie = (1.0 / z[0:1, :] for z in (za, zc, zb, ze))

    only_k = jnp.where(lane < TD, 0.0, q[:, :128])
    only_v = pltpu.roll(jnp.where(lane < TD, 0.0, q[:, 128:]), 64, 1)
    wd = jnp.concatenate([only_k, only_v], axis=0).astype(BF16)

    def grads(i, acc):
        here = pl.ds(pl.multiple_of(i * second, second), second)
        gk = (e_ref[here, 128:256] * ic - e_ref[here, 0:128] * ia).astype(BF16)
        gv = (e_ref[here, 384:512] * ie - e_ref[here, 256:384] * ib).astype(BF16)
        g = jnp.concatenate([gk, gv], axis=1)
        dk_ref[here, :] += jnp.dot(g, wd, preferred_element_type=F32)
        return acc + jnp.dot(kt_ref[:, here], g, preferred_element_type=F32)

    acc = lax.fori_loop(0, count // second, grads, jnp.zeros((128, 256), F32))
    d = jnp.where(row < TD, acc[:, RB:], acc[:, :RB])
    dq_ref[...] = d.T * sscale

    @pl.when(pl.program_id(1) == pl.num_programs(1) - 1)
    def _():
        last = lax.broadcasted_iota(jnp.int32, (1, 128), 1) == 127

        def finish(i, _):
            here = pl.ds(pl.multiple_of(i * second, second), second)
            dk_ref[here, :] = jnp.where(last, kl_ref[0, 0], dk_ref[here, :] * sscale)
            return 0

        lax.fori_loop(0, count // second, finish, 0)


def relation(q, k, valid):
    rows, count = q.shape[0], k.shape[0]
    local_heads = q.shape[1] // 256
    return pl.pallas_call(
        functools.partial(kernel, valid),
        out_shape=(
            jax.ShapeDtypeStruct((rows, local_heads * 128), F32),
            jax.ShapeDtypeStruct((count, local_heads * 128), F32),
        ),
        grid_spec=pltpu.PrefetchScalarGridSpec(
            num_scalar_prefetch=0,
            grid=(local_heads, rows // RB),
            in_specs=[
                pl.BlockSpec((RB, 256), lambda h, r: (r, h)),
                pl.BlockSpec((count, 256), lambda h, r: (0, h)),
            ],
            out_specs=[
                pl.BlockSpec((RB, 128), lambda h, r: (r, h)),
                pl.BlockSpec((count, 128), lambda h, r: (0, h)),
            ],
            scratch_shapes=[
                pltpu.VMEM((128, count), BF16),
                pltpu.VMEM((8, 256), F32),
                pltpu.VMEM((count, 512), F32),
                pltpu.VMEM((6, 8, RB), F32),
                pltpu.SMEM((1, 1), F32),
            ],
        ),
        compiler_params=pltpu.CompilerParams(
            dimension_semantics=("arbitrary", "arbitrary"), vmem_limit_bytes=52 << 20
        ),
        cost_estimate=pl.CostEstimate(
            flops=int(local_heads * rows * count * 2 * 1024),
            bytes_accessed=int(local_heads * count * 1024),
            transcendentals=int(local_heads * rows * count * 4),
        ),
    )(q, k)


def on_device(teacher_query, teacher_key, teacher_value, student_query, student_key, student_value):
    tokens = teacher_query.shape[0]
    blank = jnp.zeros((tokens, 128 - TD - SD), BF16)
    pairs = (
        (teacher_query, student_query),
        (teacher_key, student_key),
        (teacher_value, student_value),
    )
    pieces = []
    for h in range(HEADS):
        for teacher, student in pairs:
            pieces += [teacher[:, h * TD : (h + 1) * TD], student[:, h * SD : (h + 1) * SD], blank]
    packed = jnp.concatenate(pieces, axis=1)
    mine = lax.all_to_all(packed, "head", split_axis=1, concat_axis=0, tiled=True)
    rows = mine.shape[0]
    local_heads = mine.shape[1] // 384
    total_rows = rows * lax.axis_size("seq")
    padded = -(-rows // RB) * RB
    shares = []
    for h in range(local_heads):
        block = mine[:, h * 384 : (h + 1) * 384]
        keys = lax.all_gather(block[:, 128:], "seq", axis=0, tiled=True)
        queries = jnp.concatenate([block[:, :128], block[:, 256:]], axis=1)
        queries = jnp.pad(queries, ((0, padded - rows), (0, 0)))
        dq, dk = relation(queries, keys, rows)
        owned = lax.psum_scatter(dk, "seq", scatter_dimension=0, tiled=True)
        loss = owned[:, 127:]
        high = loss.astype(BF16)
        low = (loss - high.astype(F32)).astype(BF16)
        dq = dq[:rows]
        grads = jnp.concatenate(
            [dq[:, TD : TD + SD], owned[:, TD : TD + SD], owned[:, :SD] + dq[:, :SD]], axis=1
        )
        shares += [grads.astype(BF16), high, low]
    out = jnp.concatenate(shares, axis=1)
    out = lax.all_to_all(out, "head", split_axis=0, concat_axis=1, tiled=True)
    width = 3 * SD + 2
    outs = tuple(
        jnp.concatenate(
            [out[:, h * width + n * SD : h * width + (n + 1) * SD] for h in range(HEADS)], axis=1
        )
        for n in range(3)
    )
    sums = [out[0, h * width + 3 * SD : (h + 1) * width].astype(F32) for h in range(HEADS)]
    loss = jnp.sum(jnp.stack(sums)) / (HEADS * total_rows)
    return outs + (loss,)


def solution(mesh):
    spec = P(("seq", "head"), None)
    return jax.shard_map(
        on_device, mesh=mesh, in_specs=(spec,) * 6, out_specs=(spec, spec, spec, P()),
        check_vma=False,
    )
```

```python
import functools
import math

import jax
import jax.numpy as jnp
from jax import lax
from jax.experimental import pallas as pl
from jax.experimental.pallas import tpu as pltpu
from jax.sharding import PartitionSpec as P

HEADS = 16
TD = 64
SD = 48
RB = 128
LIMIT = 100.0
LOG2E = math.log2(math.e)
LN2 = math.log(2.0)
F32 = jnp.float32
BF16 = jnp.bfloat16


def pick(count, options):
    for size in options:
        if count % size == 0:
            return size
    return count


def fold(x):
    return jnp.sum(x.reshape(x.shape[0] // 8, 8, x.shape[1]), axis=0)


def fold_max(x):
    return jnp.max(x.reshape(x.shape[0] // 8, 8, x.shape[1]), axis=0)


def kernel(rows, q_ref, k_ref, dq_ref, out_ref, kt_ref, cm_ref, e_ref, st_ref, kl_ref, dk_ref):
    count = k_ref.shape[0]
    first = pick(count, (1792, 1024, 512, 256, 128))
    second = pick(count, (3584, 1024, 512, 256, 128))
    tfac = TD ** (-0.5) * LOG2E
    sfac = SD ** (-0.5) * LOG2E
    sscale = SD ** (-0.5)

    @pl.when(pl.program_id(1) == 0)
    def _():
        dk_ref[...] = jnp.zeros_like(dk_ref)
        part = pick(count, (1024, 512, 256, 128))

        def prepare(i, tops):
            here = pl.ds(pl.multiple_of(i * part, part), part)
            x = k_ref[here, :].astype(F32)
            kt_ref[64:128, here] = x[:, :128].T[64:, :].astype(BF16)
            kt_ref[0:64, here] = x[:, 128:].T[64:, :].astype(BF16)
            return jnp.maximum(tops, fold_max(jnp.abs(x)))

        tops = lax.fori_loop(0, count // part, prepare, jnp.zeros((8, 256), F32))
        tops = jnp.max(tops, axis=0, keepdims=True)
        cm_ref[...] = jnp.broadcast_to(tops, cm_ref.shape)

    q = q_ref[...].astype(F32)
    lane = lax.broadcasted_iota(jnp.int32, (RB, 128), 1)
    row = lax.broadcasted_iota(jnp.int32, (128, RB), 0)

    def weights(block):
        t = block.T
        t = jnp.concatenate(
            [jnp.where(row < TD, t, 0.0), jnp.where(row < TD, 0.0, t)], axis=1
        )
        return t

    raw_k, raw_v = weights(q[:, :128]), weights(q[:, 128:])
    col = lax.broadcasted_iota(jnp.int32, (1, 256), 1)
    factor = jnp.where(col < RB, tfac, sfac)
    full_k, full_v = raw_k * factor, raw_v * factor
    bound_k = jnp.dot(
        cm_ref[:, :128].astype(BF16), jnp.abs(raw_k).astype(BF16), preferred_element_type=F32
    )
    bound_v = jnp.dot(
        cm_ref[:, 128:].astype(BF16), jnp.abs(raw_v).astype(BF16), preferred_element_type=F32
    )
    bound = jnp.max(jnp.maximum(bound_k * factor, bound_v * factor))

    zero = jnp.zeros((8, RB), F32)

    def total(x):
        return jnp.broadcast_to(jnp.sum(x, axis=0, keepdims=True), x.shape)

    @pl.when(bound <= LIMIT)
    def _():
        def split(w):
            high = w.astype(BF16)
            low = (w - high.astype(F32)).astype(BF16)
            return jnp.concatenate([high, low], axis=0)

        wk, wv = split(full_k), split(full_v)

        def step(i, carry):
            za, zc, s, zb, ze, u = carry
            here = pl.ds(pl.multiple_of(i * first, first), first)
            xk = k_ref[here, :128]
            xv = k_ref[here, 128:]
            lk = jnp.dot(jnp.concatenate([xk, xk], axis=1), wk, preferred_element_type=F32)
            lv = jnp.dot(jnp.concatenate([xv, xv], axis=1), wv, preferred_element_type=F32)
            a, c, b, e = lk[:, :RB], lk[:, RB:], lv[:, :RB], lv[:, RB:]
            pa, pc, pb, pe = jnp.exp2(a), jnp.exp2(c), jnp.exp2(b), jnp.exp2(e)
            e_ref[here, 0:128] = pa.astype(e_ref.dtype)
            e_ref[here, 128:256] = pc.astype(e_ref.dtype)
            e_ref[here, 256:384] = pb.astype(e_ref.dtype)
            e_ref[here, 384:512] = pe.astype(e_ref.dtype)
            return (
                za + fold(pa), zc + fold(pc), s + fold(pa * (a - c)),
                zb + fold(pb), ze + fold(pe), u + fold(pb * (b - e)),
            )

        out = lax.fori_loop(0, count // first, step, (zero,) * 6)
        for n, value in enumerate(out):
            st_ref[n] = total(value)

    @pl.when(jnp.logical_not(bound <= LIMIT))
    def _():
        wk, wv = raw_k.astype(BF16), raw_v.astype(BF16)

        def blocks(i):
            here = pl.ds(pl.multiple_of(i * first, first), first)
            lk = jnp.dot(k_ref[here, :128], wk, preferred_element_type=F32)
            lv = jnp.dot(k_ref[here, 128:], wv, preferred_element_type=F32)
            return here, (
                lk[:, :RB] * tfac, lk[:, RB:] * sfac, lv[:, :RB] * tfac, lv[:, RB:] * sfac
            )

        def peak(i, tops):
            _, parts = blocks(i)
            return tuple(jnp.maximum(t, fold_max(p)) for t, p in zip(tops, parts))

        tops = lax.fori_loop(
            0, count // first, peak, (jnp.full((8, RB), -3e38, F32),) * 4
        )
        tops = tuple(jnp.max(t, axis=0, keepdims=True) for t in tops)

        def step(i, carry):
            za, zc, s, zb, ze, u = carry
            here, parts = blocks(i)
            a, c, b, e = (p - t for p, t in zip(parts, tops))
            pa, pc, pb, pe = jnp.exp2(a), jnp.exp2(c), jnp.exp2(b), jnp.exp2(e)
            e_ref[here, 0:128] = pa.astype(e_ref.dtype)
            e_ref[here, 128:256] = pc.astype(e_ref.dtype)
            e_ref[here, 256:384] = pb.astype(e_ref.dtype)
            e_ref[here, 384:512] = pe.astype(e_ref.dtype)
            return (
                za + fold(pa), zc + fold(pc), s + fold(pa * (a - c)),
                zb + fold(pb), ze + fold(pe), u + fold(pb * (b - e)),
            )

        out = lax.fori_loop(0, count // first, step, (zero,) * 6)
        for n, value in enumerate(out):
            st_ref[n] = total(value)

    za, zc, s, zb, ze, u = (st_ref[n] for n in range(6))
    kl = (s / za - jnp.log2(za) + jnp.log2(zc) + u / zb - jnp.log2(zb) + jnp.log2(ze)) * LN2
    place = pl.program_id(1) * RB + lax.broadcasted_iota(jnp.int32, (8, RB), 1)
    kl = jnp.sum(jnp.where(place < rows, kl, 0.0)) * 0.125
    kl_ref[0, 0] = jnp.where(pl.program_id(1) == 0, 0.0, kl_ref[0, 0]) + kl
    ia, ic, ib, ie = (1.0 / z[0:1, :] for z in (za, zc, zb, ze))

    only_k = jnp.where(lane < TD, 0.0, q[:, :128])
    only_v = pltpu.roll(jnp.where(lane < TD, 0.0, q[:, 128:]), 64, 1)
    wd = jnp.concatenate([only_k, only_v], axis=0).astype(BF16)

    def grads(i, acc):
        here = pl.ds(pl.multiple_of(i * second, second), second)
        gk = (e_ref[here, 128:256] * ic - e_ref[here, 0:128] * ia).astype(BF16)
        gv = (e_ref[here, 384:512] * ie - e_ref[here, 256:384] * ib).astype(BF16)
        g = jnp.concatenate([gk, gv], axis=1)
        dk_ref[here, :] += jnp.dot(g, wd, preferred_element_type=F32)
        return acc + jnp.dot(kt_ref[:, here], g, preferred_element_type=F32)

    acc = lax.fori_loop(0, count // second, grads, jnp.zeros((128, 256), F32))
    d = jnp.where(row < TD, acc[:, RB:], acc[:, :RB])
    dq_ref[...] = d.T * sscale

    @pl.when(pl.program_id(1) == pl.num_programs(1) - 1)
    def _():
        spot = lax.broadcasted_iota(jnp.int32, (1, 128), 1)
        rank = lax.axis_index("seq")
        loss = jnp.full((1, 128), kl_ref[0, 0], F32)
        high = loss.astype(BF16).astype(F32)
        extra = jnp.where(spot < TD, high, loss - high)
        mark = jnp.logical_or(spot == SD + rank, spot == TD + SD + rank)

        def finish(i, _):
            here = pl.ds(pl.multiple_of(i * second, second), second)
            out_ref[here, :] = jnp.where(mark, extra, dk_ref[here, :] * sscale).astype(BF16)
            return 0

        lax.fori_loop(0, count // second, finish, 0)


def relation(q, k, valid):
    rows, count = q.shape[0], k.shape[0]
    local_heads = q.shape[1] // 256
    return pl.pallas_call(
        functools.partial(kernel, valid),
        out_shape=(
            jax.ShapeDtypeStruct((rows, local_heads * 128), F32),
            jax.ShapeDtypeStruct((count, local_heads * 128), BF16),
        ),
        grid_spec=pltpu.PrefetchScalarGridSpec(
            num_scalar_prefetch=0,
            grid=(local_heads, rows // RB),
            in_specs=[
                pl.BlockSpec((RB, 256), lambda h, r: (r, h)),
                pl.BlockSpec((count, 256), lambda h, r: (0, h)),
            ],
            out_specs=[
                pl.BlockSpec((RB, 128), lambda h, r: (r, h)),
                pl.BlockSpec((count, 128), lambda h, r: (0, h)),
            ],
            scratch_shapes=[
                pltpu.VMEM((128, count), BF16),
                pltpu.VMEM((8, 256), F32),
                pltpu.VMEM((count, 512), F32),
                pltpu.VMEM((6, 8, RB), F32),
                pltpu.SMEM((1, 1), F32),
                pltpu.VMEM((count, 128), F32),
            ],
        ),
        compiler_params=pltpu.CompilerParams(
            dimension_semantics=("arbitrary", "arbitrary"), vmem_limit_bytes=52 << 20
        ),
        cost_estimate=pl.CostEstimate(
            flops=int(local_heads * rows * count * 2 * 1024),
            bytes_accessed=int(local_heads * count * 1024),
            transcendentals=int(local_heads * rows * count * 4),
        ),
    )(q, k)


def on_device(teacher_query, teacher_key, teacher_value, student_query, student_key, student_value):
    tokens = teacher_query.shape[0]
    blank = jnp.zeros((tokens, 128 - TD - SD), BF16)
    pairs = (
        (teacher_query, student_query),
        (teacher_key, student_key),
        (teacher_value, student_value),
    )
    pieces = []
    for h in range(HEADS):
        for teacher, student in pairs:
            pieces += [teacher[:, h * TD : (h + 1) * TD], student[:, h * SD : (h + 1) * SD], blank]
    packed = jnp.concatenate(pieces, axis=1)
    mine = lax.all_to_all(packed, "head", split_axis=1, concat_axis=0, tiled=True)
    rows = mine.shape[0]
    local_heads = mine.shape[1] // 384
    total_rows = rows * lax.axis_size("seq")
    padded = -(-rows // RB) * RB
    shares = []
    for h in range(local_heads):
        block = mine[:, h * 384 : (h + 1) * 384]
        keys = lax.all_gather(block[:, 128:], "seq", axis=0, tiled=True)
        queries = jnp.concatenate([block[:, :128], block[:, 256:]], axis=1)
        queries = jnp.pad(queries, ((0, padded - rows), (0, 0)))
        dq, dk = relation(queries, keys, rows)
        owned = lax.psum_scatter(dk, "seq", scatter_dimension=0, tiled=True)
        owned = owned.astype(F32)
        loss = jnp.sum(owned[:, SD:TD], axis=1, keepdims=True)
        loss = loss + jnp.sum(owned[:, TD + SD :], axis=1, keepdims=True)
        high = loss.astype(BF16)
        low = (loss - high.astype(F32)).astype(BF16)
        dq = dq[:rows]
        grads = jnp.concatenate(
            [dq[:, TD : TD + SD], owned[:, TD : TD + SD], owned[:, :SD] + dq[:, :SD]], axis=1
        )
        shares += [grads.astype(BF16), high, low]
    out = jnp.concatenate(shares, axis=1)
    out = lax.all_to_all(out, "head", split_axis=0, concat_axis=1, tiled=True)
    width = 3 * SD + 2
    outs = tuple(
        jnp.concatenate(
            [out[:, h * width + n * SD : h * width + (n + 1) * SD] for h in range(HEADS)], axis=1
        )
        for n in range(3)
    )
    sums = [out[0, h * width + 3 * SD : (h + 1) * width].astype(F32) for h in range(HEADS)]
    loss = jnp.sum(jnp.stack(sums)) / (HEADS * total_rows)
    return outs + (loss,)


def solution(mesh):
    spec = P(("seq", "head"), None)
    return jax.shard_map(
        on_device, mesh=mesh, in_specs=(spec,) * 6, out_specs=(spec, spec, spec, P()),
        check_vma=False,
    )
```
